32 devices in a mesh: rep: 2 (over x), group: 4 (over z), proto: 4 (over y, core).
Axes of the slice: x: 2, y: 2, z: 4, core: 2. Of those that a mesh axis runs over, the one named last changes fastest.
Arguments:
- embeddings: bfloat16 [16384, 768], P(('rep', 'group')), may hold values from -6 to 6
- labels: int32 [16384], P(('rep', 'group')), may hold values from 0 to 255, as said below
- cluster_place: int32 [256], replicated, may hold values from 0 to 255, as said below
- row_counts: int32 [8], P(('rep', 'group')), may hold values from 1536 to 2048, as said below
- prototypes: bfloat16 [256, 64, 768], P('group', 'proto'), may hold values from -6 to 6
Outputs:
- new_prototypes: float32 [256, 64, 768], P('group', 'proto', 'rep')
- codes: float32 [16384, 64], P(('rep', 'group'), 'proto')
The draws below stay inside these ranges and needn't reach their ends.
Inputs may be any that keep to these rules, and one draw needn't show every extreme that they name: Among the live rows of one block of 2048 rows, at most 1024 have labels whose place lies in any one group (place // 64); in every draw some group gets exactly 1024 live rows from every block. `cluster_place`: A permutation of the coarse clusters. `row_counts`: rows of a block at positions of its count and beyond are padding.
All inputs are finite; a program needn't handle non-finite values.
Results may differ from the reference program's by a relative error of at most 0.0042.
Values may be sent and summed in bfloat16 or wider, within the bound.
A program may use at most 128 MiB of HBM per device.

```python
import jax
import jax.numpy as jnp
from jax import lax

VECTOR_LENGTH = 768
CPG = 64
FPC = 64
ROW_DEV = 2048
ITERS = 3
TOP_GROUP_TOTAL = 256
ROWS = 16384
N_REP = 2
N_GROUP = 4


def joint_draw(key):
    base = jax.random.fold_in(key, 7)
    key_perm, key_count, key_first, key_hot, key_order, key_slot = jax.random.split(base, 6)
    place_map = jax.random.permutation(key_perm, TOP_GROUP_TOTAL).astype(jnp.int32)
    inverse = jnp.argsort(place_map).astype(jnp.int32)
    blocks = N_REP * N_GROUP
    counts = jax.random.randint(key_count, (blocks,), 3 * ROW_DEV // 4, ROW_DEV + 1).astype(jnp.int32)
    first_block = jax.random.randint(key_first, (), 0, blocks)
    counts = counts.at[first_block].set(ROW_DEV)
    counts = counts.at[(first_block + 1) % blocks].set(3 * ROW_DEV // 4)
    hot_group = jax.random.randint(key_hot, (), 0, N_GROUP).astype(jnp.int32)
    capacity = ROW_DEV // max(N_GROUP // 4, 2)
    position = jnp.arange(ROW_DEV, dtype=jnp.int32)
    template = jnp.where(position < capacity, hot_group, (hot_group + 1 + (position - capacity) % (N_GROUP - 1)) % N_GROUP)
    noise = jax.random.randint(key_order, (blocks, ROW_DEV), 0, 2 ** 30 // ROW_DEV).astype(jnp.int32)
    similarity_matrix = jnp.where(position[None, :] < counts[:, None], noise * ROW_DEV + position[None, :], 2 ** 30 + position[None, :])
    order = jnp.argsort(similarity_matrix, axis=1, stable=True)
    target = template[order]
    slot_pick = jax.random.randint(key_slot, (blocks, ROW_DEV), 0, CPG).astype(jnp.int32)
    labels = inverse[target * CPG + slot_pick].reshape(ROWS)
    return (place_map, labels.astype(jnp.int32), counts)


def draw_labels(key, part):
    return joint_draw(key)[1]


def draw_cluster_place(key, part):
    return joint_draw(key)[0]


def draw_row_counts(key, part):
    return joint_draw(key)[2]


def level_of(rng, shape, cuts, least, high):
    loudness, own = 1.0, jax.random.fold_in(rng, 6)
    for axis_at, shards_of in cuts:
        steps = jnp.exp(jax.random.uniform(jax.random.fold_in(own, axis_at), (shards_of,), jnp.float32, least / len(cuts), high / len(cuts)))
        loudness = loudness * jnp.repeat(steps, shape[axis_at] // shards_of).reshape([-1 if axis == axis_at else 1 for axis in range(len(shape))])
    return loudness


def normal_values(stream_key, dims, scale, bound, cuts=(), held_as=jnp.bfloat16):
    gain = level_of(stream_key, dims, cuts, -0.22, 0.18) if cuts else 1.0
    values = jax.random.normal(stream_key, dims, jnp.float32) * scale * gain
    return jnp.minimum(jnp.maximum(values, -bound), bound).astype(held_as)


def setup_inputs(seed: int = 0) -> dict:
    keys = jax.random.split(jax.random.key(seed), 6)
    embeddings = normal_values(keys[0], (ROWS, VECTOR_LENGTH), 1.0, 6.0, ((0, 8),))
    labels = draw_labels(jax.random.fold_in(keys[5], 71), 0)
    cluster_place = draw_cluster_place(jax.random.fold_in(keys[5], 71), 0)
    row_counts = draw_row_counts(jax.random.fold_in(keys[5], 71), 0)
    prototypes = normal_values(keys[4], (TOP_GROUP_TOTAL, FPC, VECTOR_LENGTH), 1.0, 6.0, ((0, 4), (1, 4)))
    return dict(embeddings=embeddings, labels=labels, cluster_place=cluster_place, row_counts=row_counts, prototypes=prototypes)


sharpness_divisor = 0.03

def unit(values):
    return values * lax.rsqrt(lax.optimization_barrier(jnp.mean(values * values, axis=-1, keepdims=True)) + 1e-06)

def reference(embeddings, labels, cluster_place, row_counts, prototypes):
    rows_f = embeddings.astype(jnp.float32)
    unit_rows = unit(rows_f).astype(jnp.bfloat16)
    proto_f = prototypes.astype(jnp.float32)
    unit_protos = unit(proto_f).astype(jnp.bfloat16)
    row_ids = jnp.arange(ROWS, dtype=jnp.int32)
    block_ids = row_ids // ROW_DEV
    live = row_ids - block_ids * ROW_DEV < row_counts[block_ids]
    present_indicator = live.astype(jnp.float32)
    sample_location = cluster_place[labels].astype(jnp.int32)
    blocks = ROWS // ROW_DEV
    unit_blocks = unit_rows.reshape(blocks, ROW_DEV, VECTOR_LENGTH)
    place_blocks = sample_location.reshape(blocks, ROW_DEV)

    def score_block(block_pair):
        rows_b, place_b = block_pair
        protos_b = unit_protos[place_b]
        return jnp.einsum('rd,rfd->rf', rows_b.astype(jnp.float32), protos_b.astype(jnp.float32))
    similarity_matrix = lax.map(score_block, (unit_blocks, place_blocks)).reshape(ROWS, FPC)
    balanced_transport_routine = present_indicator[:, None] * jnp.exp(similarity_matrix * (1.0 / (VECTOR_LENGTH * sharpness_divisor)))
    count = jax.ops.segment_sum(present_indicator, sample_location, num_segments=TOP_GROUP_TOTAL)
    occupied = count[:, None] > 0
    sample_importance = present_indicator
    normalizer_factor = jnp.zeros((TOP_GROUP_TOTAL, FPC), jnp.float32)
    for iteration in range(ITERS):
        target_entry = jax.ops.segment_sum(balanced_transport_routine * sample_importance[:, None], sample_location, num_segments=TOP_GROUP_TOTAL)
        normalizer_factor = jnp.where(occupied, count[:, None] / FPC / jnp.where(occupied, target_entry, 1.0), 0.0)
        sample_total = lax.optimization_barrier(jnp.sum(balanced_transport_routine * normalizer_factor[sample_location], axis=1))
        sample_importance = jnp.where(live, 1.0 / jnp.where(live, sample_total, 1.0), 0.0)
    transport_matrix = sample_importance[:, None] * balanced_transport_routine * normalizer_factor[sample_location]
    codes = FPC * transport_matrix
    plan_low = transport_matrix.astype(jnp.bfloat16)
    col_mass = jax.ops.segment_sum(transport_matrix, sample_location, num_segments=TOP_GROUP_TOTAL)
    plan_blocks = plan_low.reshape(blocks, ROW_DEV, FPC)

    def add_block(moment, block_triple):
        plan_b, rows_b, place_b = block_triple
        outer = jnp.einsum('rf,rd->rfd', plan_b.astype(jnp.float32), rows_b.astype(jnp.float32))
        return (moment.at[place_b].add(outer), None)
    moment, unused = lax.scan(add_block, jnp.zeros((TOP_GROUP_TOTAL, FPC, VECTOR_LENGTH), jnp.float32), (plan_blocks, unit_blocks, place_blocks))
    updated = (proto_f + moment) / (1.0 + col_mass[:, :, None])
    new_prototypes = updated * lax.rsqrt(lax.optimization_barrier(jnp.mean(updated * updated, axis=-1, keepdims=True)) + 1e-06)
    return (new_prototypes, codes)
```

```python
import functools

import jax
import jax.numpy as jnp
from jax import lax
from jax.experimental import pallas as pl
from jax.experimental.pallas import tpu as pltpu
from jax.sharding import PartitionSpec as P

FPC = 64
ITERS = 3
SHARPNESS = 0.03
EXTRA = 16
F32, BF16 = jnp.float32, jnp.bfloat16
MESH = pl.DeviceIdType.MESH
VM = pl.BlockSpec(memory_space=pltpu.VMEM)
NT = (((1,), (1,)), ((), ()))


def unit(values):
    return values * lax.rsqrt(jnp.mean(values * values, axis=-1, keepdims=True) + 1e-06)


def remote(src, dst, send_sem, recv_sem, where):
    return pltpu.make_async_remote_copy(
        src_ref=src, dst_ref=dst, send_sem=send_sem, recv_sem=recv_sem,
        device_id=where, device_id_type=MESH)


def greet(peers):
    barrier = pltpu.get_barrier_semaphore()
    for peer in peers:
        pl.semaphore_signal(barrier, inc=1, device_id=peer, device_id_type=MESH)
    pl.semaphore_wait(barrier, len(peers))


def others(name):
    n, me = lax.axis_size(name), lax.axis_index(name)
    return [{name: lax.rem(me + k, n)} for k in range(1, n)]


def dispatch_kernel(groups, protos, cap, tile, width, dest_ref, slot_ref, xa_ref, xb_ref, w_ref,
                    got_ref, gotw_ref, send, ssem, rsem, wssem, wrsem, lsem):
    me, mp = lax.axis_index("group"), lax.axis_index("proto")
    half = cap // 2
    wide = xa_ref.shape[1]
    off = width - wide
    greet(others("group") + others("proto"))
    wcopies = []
    for k in range(1, protos):
        to = lax.rem(mp + k, protos)
        c = remote(w_ref.at[to], gotw_ref.at[mp], wssem.at[k], wrsem.at[k], {"proto": to})
        c.start()
        wcopies.append(c)
    own = pltpu.make_async_copy(w_ref.at[mp], gotw_ref.at[mp], lsem)
    own.start()
    copies = []
    rows = dest_ref.shape[1]
    row16 = lax.broadcasted_iota(jnp.int32, (EXTRA, tile), 0)
    order = [groups // 2] + [k for k in range(1, groups) if k != groups // 2] + [0]
    for k in order:
        to = lax.rem(me + k, groups)

        buf = got_ref.at[me] if k == 0 else send.at[k]
        codes = jnp.zeros((EXTRA, tile), F32)
        for t in range(half // tile):
            at = lax.broadcasted_iota(jnp.int32, (tile, rows), 0) + (to * cap + t * tile)
            oa = jnp.where(at == dest_ref[...], 1.0, 0.0).astype(BF16)
            ob = jnp.where(at + half == dest_ref[...], 1.0, 0.0).astype(BF16)
            a = jnp.dot(oa, xa_ref[...], preferred_element_type=F32)
            b = jnp.dot(ob, xb_ref[...], preferred_element_type=F32)
            sa = lax.dot_general(slot_ref[...], oa, NT, preferred_element_type=F32)
            sb = lax.dot_general(slot_ref[...], ob, NT, preferred_element_type=F32)
            codes = jnp.where(row16 == t, sa, codes)
            codes = jnp.where(row16 == half // tile + t, sb, codes)
            r = pl.ds(t * tile, tile)
            buf[r, :off] = a[:, :off].astype(BF16)
            buf[r, off:wide] = (a[:, off:] + b[:, :wide - off]).astype(BF16)
            buf[r, wide:] = b[:, wide - off:].astype(BF16)
        buf[pl.ds(half, EXTRA), :tile] = codes.astype(BF16)
        buf[pl.ds(half, EXTRA), tile:] = jnp.zeros((EXTRA, width - tile), BF16)
        if k:
            c = remote(send.at[k], got_ref.at[me], ssem.at[k], rsem.at[k], {"group": to})
            c.start()
            copies.append(c)
    own.wait()
    for c in wcopies + copies:
        c.wait()


def sinkhorn_kernel(groups, protos, reps, cap, tile, scale, got_ref, w_ref,
                    plan_ref, mass_ref, slot_ref, r_ref,
                    part, prec, member, xs, xr, kall,
                    psem, prsem, ksem, krsem, xsem, xrsem):
    mp, mr = lax.axis_index("proto"), lax.axis_index("rep")
    half = cap // 2
    total = groups * cap
    width = got_ref.shape[2]
    wide = r_ref.shape[1]
    off = width - wide
    cols = w_ref.shape[1]
    fine = FPC // protos
    clusters = cols // fine
    greet(others("proto") + others("rep"))
    for g in range(groups):
        a = got_ref[g, :half, :wide]
        b = got_ref[g, :half, off:].astype(F32)
        r_ref[pl.ds(g * cap, half), :] = a
        r_ref[pl.ds(g * cap + half, half), :] = pltpu.roll(b, wide - (width // 2 - off), 1).astype(BF16)
        for u in range(cap // tile):
            s = got_ref[g, pl.ds(half, EXTRA), :tile].astype(F32)[u:u + 1, :]
            slot_ref[:, pl.ds(g * cap + u * tile, tile)] = jnp.broadcast_to(s, (8, tile)).astype(jnp.int32)

    chunk = 512
    step = 256
    per = step // fine

    def score(to, c):
        lanes = pl.ds(pl.multiple_of(c * chunk, chunk), chunk)
        rows = r_ref[lanes, :]
        slots = jnp.broadcast_to(slot_ref[:1, lanes], (fine, chunk))
        acc = jnp.zeros((fine, chunk), F32)
        for j in range(cols // step):
            s = lax.dot_general(w_ref[to, pl.ds(j * step, step), :], rows, NT, preferred_element_type=F32)
            for i in range(per):
                acc = jnp.where(slots == j * per + i + 1, s[i * fine:(i + 1) * fine], acc)
        return lanes, acc

    copies = []
    for k in list(range(1, protos)) + [0]:
        to = lax.rem(mp + k, protos)

        @pl.loop(0, total // chunk)
        def _(c):
            lanes, acc = score(to, c)
            part[k, :, lanes] = acc

        if k:
            c = remote(part.at[k], prec.at[k], psem.at[k], prsem.at[k], {"proto": to})
            c.start()
            copies.append(c)
    for c in copies:
        c.wait()
    live = slot_ref[:1, :] > 0
    s = part[0]
    for k in range(1, protos):
        s = s + prec[k]
    kern = jnp.where(live, jnp.exp(s * scale), 0.0).astype(BF16)
    kall[mp] = kern
    copies = []
    for k in range(1, protos):
        to = lax.rem(mp + k, protos)
        c = remote(kall.at[mp], kall.at[mp], ksem.at[k], krsem.at[k], {"proto": to})
        c.start()
        copies.append(c)
    width_m = member.shape[0]
    cl = lax.broadcasted_iota(jnp.int32, (width_m, chunk), 0) + 1

    @pl.loop(0, total // chunk)
    def _(c):
        lanes = pl.ds(pl.multiple_of(c * chunk, chunk), chunk)
        member[:, lanes] = jnp.where(slot_ref[:1, lanes] == cl, 1.0, 0.0).astype(BF16)

    for c in copies:
        c.wait()

    def exchange(n, value):
        xs[n] = value
        cs = []
        for k in range(1, reps):
            to = lax.rem(mr + k, reps)
            c = remote(xs.at[n], xr.at[n, k], xsem.at[n, k], xrsem.at[n, k], {"rep": to})
            c.start()
            cs.append(c)
        for k in range(1, reps):
            cs[k - 1].wait()
            value = value + xr[n, k]
        return value

    def pad8(v):
        return jnp.concatenate([v, jnp.zeros((8, width_m), F32)], axis=0)

    nch = total // chunk
    livef = live.astype(F32)

    def piece(c):
        return slice(c * chunk, (c + 1) * chunk)

    def kern_of(c):
        return kall[:, :, piece(c)].reshape(FPC, chunk).astype(F32)

    weights = [livef[:, piece(c)] for c in range(nch)]
    counts = lax.dot_general(jnp.broadcast_to(livef, (16, total)).astype(BF16), member[...], NT,
                             preferred_element_type=F32)[:8]
    for n in range(ITERS):
        col = jnp.zeros((FPC, width_m), F32)
        for c in range(nch):
            kw = (kern_of(c) * weights[c]).astype(BF16)
            col = col + lax.dot_general(kw, member[:, piece(c)], NT, preferred_element_type=F32)
        if n == 0:
            both = exchange(0, jnp.concatenate([col, counts], axis=0))
            col, count = both[:FPC], both[FPC:FPC + 1]
        else:
            col = exchange(n, pad8(col))[:FPC]
        occ = jnp.broadcast_to(count, col.shape) > 0
        scal = jnp.where(occ, count / FPC / jnp.where(occ, col, 1.0), 0.0)
        hi = scal.astype(BF16)
        lo = (scal - hi.astype(F32)).astype(BF16)
        mass = jnp.zeros((FPC, width_m), F32)
        for c in range(nch):
            m = member[:, piece(c)]
            sw = jnp.dot(hi, m, preferred_element_type=F32) + jnp.dot(lo, m, preferred_element_type=F32)
            ks = kern_of(c) * sw
            row = jnp.sum(ks, axis=0, keepdims=True)
            lv = livef[:, piece(c)] > 0
            weights[c] = jnp.where(lv, 1.0 / jnp.where(lv, row, 1.0), 0.0)
            if n == ITERS - 1:
                low = (ks * weights[c]).astype(BF16)
                plan_ref[:, piece(c)] = low
                mass = mass + lax.dot_general(low, m, NT, preferred_element_type=F32)
    mass_ref[...] = exchange(ITERS, pad8(mass))[:FPC]


def update_kernel(groups, protos, reps, cap, fw, plan_ref, slot_ref, r_ref, mass_ref, proto_ref, dest_ref,
                  new_ref, codes_ref, send, mrec, crec, ss, ssr,
                  csem, crsem, msem, mrsem, lsem, ssem, ssrsem):
    mg, mp, mr = lax.axis_index("group"), lax.axis_index("proto"), lax.axis_index("rep")
    total = groups * cap
    fine = FPC // protos
    packed = send.shape[1]
    width = send.shape[2]
    wide = r_ref.shape[1]
    off = width - wide
    shift = width // 2 - off
    share = protos // reps
    half_to = lax.rem(mp, reps)
    j_mine = mp // reps
    peers = others("group")
    for a in range(reps):
        for b in range(protos):
            if a or b:
                peers.append({"rep": lax.rem(mr + a, reps), "proto": lax.rem(mp + b, protos)})
    greet(peers)
    copies = []
    f_rows = pl.ds(pl.multiple_of(mp * fine, fine), fine)
    for k in range(1, groups):
        to = lax.rem(mg + k, groups)
        c = remote(plan_ref.at[f_rows, pl.ds(pl.multiple_of(to * cap, cap), cap)], crec.at[mg],
                   csem.at[k], crsem.at[k], {"group": to})
        c.start()
        copies.append(c)
    crec_own = plan_ref[f_rows, pl.ds(pl.multiple_of(mg * cap, cap), cap)]
    crec[mg] = crec_own

    block = 256
    per = block // fine
    chunk = 1024
    lane = lax.broadcasted_iota(jnp.int32, (block, off), 1)

    def moment(to, first):
        plan_rows = pl.ds(pl.multiple_of(to * fine, fine), fine)
        acc = jnp.zeros((block, wide), F32)
        for c in range(total // chunk):
            lanes = slice(c * chunk, (c + 1) * chunk)
            plan = plan_ref[plan_rows, lanes].astype(F32)
            slots = jnp.broadcast_to(slot_ref[:1, lanes], (fine, chunk)) - first
            a = jnp.concatenate(
                [jnp.where(slots == i + 1, plan, 0.0).astype(BF16) for i in range(per)], axis=0)
            acc = acc + jnp.dot(a, r_ref[lanes, :], preferred_element_type=F32)
        return acc

    slot_out = mr * share + j_mine
    is_self = half_to == mr
    mcopies = []
    for k in list(range(1, protos)) + [0]:
        to = lax.rem(mp + k, protos)

        @pl.loop(0, packed // block)
        def _(t):
            a = moment(to, t * per)
            b = pltpu.roll(moment(to, t * per + packed // fine), shift, 1)
            r = pl.ds(pl.multiple_of(t * block, block), block)
            send[k, r, :off] = a[:, :off].astype(BF16)
            send[k, r, off:wide] = jnp.where(lane < shift, a[:, off:], b[:, :wide - off]).astype(BF16)
            send[k, r, wide:] = b[:, wide - off:].astype(BF16)

        c = remote(send.at[k], mrec.at[slot_out], msem.at[k], mrsem.at[slot_out],
                   {"rep": half_to, "proto": to})
        if k:
            c.start()
            mcopies.append(c)
        else:
            @pl.when(is_self)
            def _():
                l = pltpu.make_async_copy(send.at[0], mrec.at[slot_out], lsem)
                l.start()
                l.wait()

            @pl.when(jnp.logical_not(is_self))
            def _():
                c.start()
                c.wait_send()

    for c in copies:
        c.wait()
    nrow = dest_ref.shape[0]
    rt = 256

    @pl.loop(0, nrow // rt)
    def _(t):
        r = pl.ds(pl.multiple_of(t * rt, rt), rt)
        acc = jnp.zeros((rt, fine), F32)
        d = jnp.broadcast_to(dest_ref[r, :], (rt, cap))
        for g in range(groups):
            hot = jnp.where(d == lax.broadcasted_iota(jnp.int32, (rt, cap), 1) + g * cap, 1.0, 0.0)
            acc = acc + lax.dot_general(hot.astype(BF16), crec[g], NT, preferred_element_type=F32)
        codes_ref[r, :] = acc * FPC

    for c in mcopies:
        c.wait_send()
    for a in range(reps):
        for j in range(share):
            s = a * share + j
            mine = jnp.logical_and(a == mr, j * reps + mr == mp)

            @pl.when(jnp.logical_not(mine))
            def _():
                remote(send.at[0], mrec.at[s], msem.at[0], mrsem.at[s],
                       {"rep": lax.rem(mr + 1, reps)}).wait_recv()

    lane2 = lax.broadcasted_iota(jnp.int32, (128, off), 1)
    eye = lax.broadcasted_iota(jnp.int32, (128, 128), 0) == lax.broadcasted_iota(jnp.int32, (128, 128), 1)
    n128 = packed // 128
    sums = []
    for t in range(n128):
        r = slice(t * 128, (t + 1) * 128)
        v = []
        for j in range(share):
            x = mrec[j, r, :].astype(F32)
            for a in range(1, reps):
                x = x + mrec[a * share + j, r, :].astype(F32)
            v.append(x)
        t0, t1 = v
        b = pltpu.roll(t1[:, :wide], shift, 1)
        u = pltpu.roll(t0[:, off:], wide - shift, 1)
        first = [t0[:, :off], jnp.where(lane2 < shift, t0[:, off:wide], b[:, :wide - off]), b[:, wide - off:]]
        second = [u[:, :off], jnp.where(lane2 < shift, u[:, off:wide], t1[:, off:wide]), t1[:, wide:]]
        for h, vals in enumerate((first, second)):
            rr = slice(h * packed + t * 128, h * packed + (t + 1) * 128)
            mom = jnp.concatenate(vals, axis=1)
            up = (proto_ref[rr, :].astype(F32) + mom) / (1.0 + mass_ref[rr, :])
            new_ref[rr, :] = up
            q = jnp.sum(up * up, axis=1, keepdims=True)
            sums.append((h * n128 + t, jnp.sum(jnp.where(eye, jnp.broadcast_to(q, (128, 128)), 0.0), axis=0, keepdims=True)))
    sums.sort(key=lambda e: e[0])
    own = jnp.concatenate([e[1] for e in sums], axis=0)
    ss[...] = own
    cs = []
    for k in range(1, reps):
        c = remote(ss, ssr.at[k], ssem.at[k], ssrsem.at[k], {"rep": lax.rem(mr + k, reps)})
        c.start()
        cs.append(c)
    for k in range(1, reps):
        cs[k - 1].wait()
        own = own + ssr[k]
    inv = lax.rsqrt(own / (fw * protos) + 1e-06)
    for t in range(2 * n128):
        rr = slice(t * 128, (t + 1) * 128)
        f = jnp.sum(jnp.where(eye, jnp.broadcast_to(inv[t:t + 1, :], (128, 128)), 0.0), axis=1, keepdims=True)
        new_ref[rr, :] = new_ref[rr, :] * f


def body(embeddings, labels, cluster_place, row_counts, prototypes):
    rows, dim = embeddings.shape
    groups, protos, reps = lax.axis_size("group"), lax.axis_size("proto"), lax.axis_size("rep")
    mp, mr = lax.axis_index("proto"), lax.axis_index("rep")
    cap = rows // max(groups // 4, 2)
    clusters, fine, _ = prototypes.shape
    share = protos // reps
    fw = dim // protos
    wide = -(-fw // 128) * 128
    width = 2 * fw
    off = width - wide
    half = cap // 2
    tile = min(256, half)
    total = groups * cap
    cols = clusters * fine

    def quarter(p):
        return (p % reps) * share + p // reps

    place = jnp.sum(jnp.where(labels[:, None] == jnp.arange(cluster_place.shape[0])[None, :],
                              cluster_place[None, :], 0), axis=1)
    target, slot = place // clusters, place % clusters
    live = jnp.arange(rows) < row_counts[0]
    choose = (target[:, None] == jnp.arange(groups)[None, :]) & live[:, None]
    running = jnp.cumsum(choose.astype(jnp.int32), axis=0) - 1
    position = jnp.sum(jnp.where(choose, running, 0), axis=1)
    dest = jnp.where(live, target * cap + position, -1).astype(jnp.int32)
    slot16 = jnp.broadcast_to((slot + 1).astype(BF16)[None, :], (16, rows))
    rows_f = embeddings.astype(F32)
    inv = lax.rsqrt(jnp.mean(rows_f * rows_f, axis=-1, keepdims=True) + 1e-06)
    q = lax.rem(mp, reps) * share + mp // reps
    mine = lax.dynamic_slice_in_dim(embeddings, q * fw, fw, 1).astype(F32)
    xq = (mine * inv).astype(BF16)
    xa = jnp.pad(xq, ((0, 0), (0, wide - fw)))
    xb = jnp.pad(xq, ((0, 0), (wide - fw, 0)))
    unit_p = unit(prototypes.astype(F32)).astype(BF16).reshape(cols, dim)
    w = jnp.stack([jnp.pad(unit_p[:, quarter(p) * fw:(quarter(p) + 1) * fw], ((0, 0), (0, wide - fw)))
                   for p in range(protos)])
    dma, sds = pltpu.SemaphoreType.DMA, jax.ShapeDtypeStruct
    params = functools.partial(pltpu.CompilerParams, has_side_effects=True, vmem_limit_bytes=60 * 2**20)
    got, gotw = pl.pallas_call(
        functools.partial(dispatch_kernel, groups, protos, cap, tile, width),
        out_shape=(sds((groups, half + EXTRA, width), BF16), sds((protos, cols, wide), BF16)),
        in_specs=[VM] * 5,
        out_specs=(VM, VM),
        scratch_shapes=[pltpu.VMEM((groups, half + EXTRA, width), BF16),
                        dma((groups,)), dma((groups,)), dma((protos,)), dma((protos,)), dma],
        compiler_params=params(collective_id=0),
    )(dest[None, :], slot16, xa, xb, w)
    plan, mass, slots, r = pl.pallas_call(
        functools.partial(sinkhorn_kernel, groups, protos, reps, cap, tile, 1.0 / (dim * SHARPNESS)),
        out_shape=(sds((FPC, total), BF16), sds((FPC, 128), F32), sds((8, total), jnp.int32),
                   sds((total, wide), BF16)),
        in_specs=[VM] * 2,
        out_specs=(VM,) * 4,
        scratch_shapes=[pltpu.VMEM((protos, fine, total), F32), pltpu.VMEM((protos, fine, total), F32),
                        pltpu.VMEM((128, total), BF16),
                        pltpu.VMEM((ITERS + 1, FPC + 8, 128), F32),
                        pltpu.VMEM((ITERS + 1, reps, FPC + 8, 128), F32),
                        pltpu.VMEM((protos, fine, total), BF16),
                        dma((protos,)), dma((protos,)), dma((protos,)), dma((protos,)),
                        dma((ITERS + 1, reps)), dma((ITERS + 1, reps))],
        compiler_params=params(collective_id=1),
    )(got, gotw)
    mass_col = lax.dynamic_slice_in_dim(mass, mp * fine, fine, 0)[:, :clusters].T.reshape(cols, 1)
    hw = dim // reps
    proto_half = lax.dynamic_slice_in_dim(prototypes, mr * hw, hw, 2).reshape(cols, hw)
    new, codes = pl.pallas_call(
        functools.partial(update_kernel, groups, protos, reps, cap, fw),
        out_shape=(sds((cols, hw), F32), sds((rows, fine), F32)),
        in_specs=[VM] * 6,
        out_specs=(VM, VM),
        scratch_shapes=[pltpu.VMEM((protos, cols // 2, width), BF16),
                        pltpu.VMEM((reps * share, cols // 2, width), BF16),
                        pltpu.VMEM((groups, fine, cap), BF16),
                        pltpu.VMEM((cols // 128, 128), F32), pltpu.VMEM((reps, cols // 128, 128), F32),
                        dma((groups,)), dma((groups,)), dma((protos,)), dma((reps * share,)), dma,
                        dma((reps,)), dma((reps,))],
        compiler_params=params(collective_id=2),
    )(plan, slots, r, mass_col, proto_half, dest[:, None])
    return new.reshape(clusters, fine, hw), codes


def solution(mesh):
    return jax.shard_map(
        body,
        mesh=mesh,
        in_specs=(
            P(("rep", "group"), None),
            P(("rep", "group")),
            P(),
            P(("rep", "group")),
            P("group", "proto", None),
        ),
        out_specs=(P("group", "proto", "rep"), P(("rep", "group"), "proto")),
        check_vma=False,
    )
```

```python
import functools

import jax
import jax.numpy as jnp
from jax import lax
from jax.experimental import pallas as pl
from jax.experimental.pallas import tpu as pltpu
from jax.sharding import PartitionSpec as P

FPC = 64
ITERS = 3
SHARPNESS = 0.03
EXTRA = 16
F32, BF16 = jnp.float32, jnp.bfloat16
MESH = pl.DeviceIdType.MESH
VM = pl.BlockSpec(memory_space=pltpu.VMEM)
NT = (((1,), (1,)), ((), ()))


def unit(values):
    return values * lax.rsqrt(jnp.mean(values * values, axis=-1, keepdims=True) + 1e-06)


def remote(src, dst, send_sem, recv_sem, where):
    return pltpu.make_async_remote_copy(
        src_ref=src, dst_ref=dst, send_sem=send_sem, recv_sem=recv_sem,
        device_id=where, device_id_type=MESH)


def greet(peers):
    barrier = pltpu.get_barrier_semaphore()
    for peer in peers:
        pl.semaphore_signal(barrier, inc=1, device_id=peer, device_id_type=MESH)
    pl.semaphore_wait(barrier, len(peers))


def others(name):
    n, me = lax.axis_size(name), lax.axis_index(name)
    return [{name: lax.rem(me + k, n)} for k in range(1, n)]


def sinkhorn_kernel(groups, protos, reps, cap, tile, width, fw, scale,
                    dest_ref, slot_in_ref, xa_ref, xb_ref, proto_ref,
                    plan_ref, mass_ref, slot_ref, r_ref,
                    got, send, wsend, wgot, w_ref, part, prec, member, xs, xr, kall,
                    ssem, rsem, wssem, wrsem, psem, prsem, ksem, krsem, xsem, xrsem):
    me, mp, mr = lax.axis_index("group"), lax.axis_index("proto"), lax.axis_index("rep")
    half = cap // 2
    total = groups * cap
    wide = r_ref.shape[1]
    off = width - wide
    shift = fw - off
    cols, dim = proto_ref.shape
    fine = FPC // protos
    share = protos // reps
    rows = dest_ref.shape[1]
    row16 = lax.broadcasted_iota(jnp.int32, (EXTRA, tile), 0)
    greet(others("group") + others("proto") + others("rep"))

    def bucket(k):
        to = lax.rem(me + k, groups)
        buf = got.at[me] if k == 0 else send.at[k]
        codes = jnp.zeros((EXTRA, tile), F32)
        for t in range(half // tile):
            at = lax.broadcasted_iota(jnp.int32, (tile, rows), 0) + (to * cap + t * tile)
            oa = jnp.where(at == dest_ref[...], 1.0, 0.0).astype(BF16)
            ob = jnp.where(at + half == dest_ref[...], 1.0, 0.0).astype(BF16)
            a = jnp.dot(oa, xa_ref[...], preferred_element_type=F32)
            b = jnp.dot(ob, xb_ref[...], preferred_element_type=F32)
            sa = lax.dot_general(slot_in_ref[...], oa, NT, preferred_element_type=F32)
            sb = lax.dot_general(slot_in_ref[...], ob, NT, preferred_element_type=F32)
            codes = jnp.where(row16 == t, sa, codes)
            codes = jnp.where(row16 == half // tile + t, sb, codes)
            r = pl.ds(t * tile, tile)
            buf[r, :off] = a[:, :off].astype(BF16)
            buf[r, off:wide] = (a[:, off:] + b[:, :wide - off]).astype(BF16)
            buf[r, wide:] = b[:, wide - off:].astype(BF16)
        buf[pl.ds(half, EXTRA), :tile] = codes.astype(BF16)
        buf[pl.ds(half, EXTRA), tile:] = jnp.zeros((EXTRA, width - tile), BF16)
        if k:
            c = remote(send.at[k], got.at[me], ssem.at[k], rsem.at[k], {"group": to})
            c.start()
            return c

    def spread_protos():
        wt = 128
        lane = lax.broadcasted_iota(jnp.int32, (wt, off), 1)

        @pl.loop(0, cols // 2 // wt)
        def _(t):
            ra = pl.ds(pl.multiple_of(t * wt, wt), wt)
            rb = pl.ds(pl.multiple_of(t * wt + cols // 2, wt), wt)
            ua, ub = unit(proto_ref[ra, :].astype(F32)), unit(proto_ref[rb, :].astype(F32))
            for q in range(protos):
                p = (q % share) * reps + q // share
                base = q * fw // 128 * 128
                o = q * fw - base
                a, b = ua[:, base:base + wide], ub[:, base:base + wide]
                a = a if o == 0 else pltpu.roll(a, wide - o, 1)
                b = b if o == shift else pltpu.roll(b, (shift - o) % wide, 1)
                wsend[p, ra, :off] = a[:, :off].astype(BF16)
                wsend[p, ra, off:wide] = jnp.where(lane < shift, a[:, off:], b[:, :wide - off]).astype(BF16)
                wsend[p, ra, wide:] = b[:, wide - off:].astype(BF16)
        cs = []
        for k in range(1, protos):
            to = lax.rem(mp + k, protos)
            c = remote(wsend.at[to], wgot.at[k], wssem.at[k], wrsem.at[k], {"proto": to})
            c.start()
            cs.append(c)
        return cs

    order = [groups // 2] + [k for k in range(1, groups) if k != groups // 2]
    sent = {order[0]: bucket(order[0])}
    wcopies = spread_protos()
    for k in order[1:]:
        sent[k] = bucket(k)
    bucket(0)

    keep = lax.broadcasted_iota(jnp.int32, (cols // 2, wide), 1) < fw
    for k in range(protos):
        if k:
            wcopies[k - 1].wait()
        src = wsend.at[mp] if k == 0 else wgot.at[k]
        w_ref[k, :cols // 2, :] = jnp.where(keep, src[:, :wide].astype(F32), 0.0).astype(BF16)
        b = pltpu.roll(src[:, off:].astype(F32), wide - shift, 1)
        w_ref[k, cols // 2:, :] = jnp.where(keep, b, 0.0).astype(BF16)

    chunk = 512
    step = 256
    per = step // fine
    width_m = member.shape[0]
    cl = lax.broadcasted_iota(jnp.int32, (width_m, cap), 0) + 1

    def lanes_of(k):
        src = lax.rem(me - k + groups, groups)
        return src, pl.ds(pl.multiple_of(src * cap, cap), cap)

    def score(k):
        src, lanes = lanes_of(k)
        if k:
            sent[k].wait()
        base = src * cap
        r_ref[pl.ds(pl.multiple_of(base, half), half), :] = got[src, :half, :wide]
        b = got[src, :half, off:].astype(F32)
        r_ref[pl.ds(pl.multiple_of(base + half, half), half), :] = pltpu.roll(b, wide - shift, 1).astype(BF16)
        codes = got[src, pl.ds(half, EXTRA), :tile].astype(F32)
        slots = jnp.concatenate([codes[u:u + 1, :] for u in range(cap // tile)], axis=1)
        slots = jnp.broadcast_to(slots, (8, cap)).astype(jnp.int32)
        slot_ref[:, lanes] = slots
        member[:, lanes] = jnp.where(slots[:1] == cl, 1.0, 0.0).astype(BF16)

        @pl.loop(0, cap // chunk)
        def _(c):
            at = pl.ds(pl.multiple_of(base + c * chunk, chunk), chunk)
            x = r_ref[at, :]
            sl = slot_ref[:, at]
            acc = [[jnp.zeros((8, chunk), F32) for _ in range(fine // 8)] for _ in range(protos)]
            for j in range(cols // step):
                for p in range(protos):
                    s = lax.dot_general(w_ref[p, j * step:(j + 1) * step, :], x, NT, preferred_element_type=F32)
                    for i in range(per):
                        hit = sl == j * per + i + 1
                        for h in range(fine // 8):
                            z = i * fine + h * 8
                            acc[p][h] = jnp.where(hit, s[z:z + 8], acc[p][h])
            for p in range(protos):
                part[p, :, at] = jnp.concatenate(acc[p], axis=0)

        cs = []
        for p in range(1, protos):
            to = lax.rem(mp - p + protos, protos)
            c = remote(part.at[p, :, lanes], prec.at[p, :, lanes], psem.at[k, p], prsem.at[k, p], {"proto": to})
            c.start()
            cs.append(c)
        return cs

    def finish(k, cs):
        _, lanes = lanes_of(k)
        for c in cs:
            c.wait()
        s = part[0, :, lanes]
        for p in range(1, protos):
            s = s + prec[p, :, lanes]
        live = jnp.broadcast_to(slot_ref[:1, lanes], s.shape) > 0
        kall[mp, :, lanes] = jnp.where(live, jnp.exp(s * scale), 0.0).astype(BF16)
        out = []
        for p in range(1, protos):
            to = lax.rem(mp + p, protos)
            c = remote(kall.at[mp, :, lanes], kall.at[mp, :, lanes], ksem.at[k, p], krsem.at[k, p], {"proto": to})
            c.start()
            out.append(c)
        return out

    pending, last = [], None
    for k in [0] + order:
        now = (k, score(k))
        if last is not None:
            pending += finish(*last)
        last = now
    pending += finish(*last)

    def exchange(n, value):
        xs[n] = value
        cs = []
        for k in range(1, reps):
            to = lax.rem(mr + k, reps)
            c = remote(xs.at[n], xr.at[n, k], xsem.at[n, k], xrsem.at[n, k], {"rep": to})
            c.start()
            cs.append(c)
        for k in range(1, reps):
            cs[k - 1].wait()
            value = value + xr[n, k]
        return value

    def pad8(v):
        return jnp.concatenate([v, jnp.zeros((8, width_m), F32)], axis=0)

    nch = total // chunk
    livef = (slot_ref[:1, :] > 0).astype(F32)

    def piece(c):
        return slice(c * chunk, (c + 1) * chunk)

    def kern_of(c):
        return kall[:, :, piece(c)].reshape(FPC, chunk).astype(F32)

    weights = [livef[:, piece(c)] for c in range(nch)]
    counts = lax.dot_general(jnp.broadcast_to(livef, (16, total)).astype(BF16), member[...], NT,
                             preferred_element_type=F32)[:8]
    for c in pending:
        c.wait()
    for n in range(ITERS):
        col = jnp.zeros((FPC, width_m), F32)
        for c in range(nch):
            kw = (kern_of(c) * weights[c]).astype(BF16)
            col = col + lax.dot_general(kw, member[:, piece(c)], NT, preferred_element_type=F32)
        if n == 0:
            both = exchange(0, jnp.concatenate([col, counts], axis=0))
            col, count = both[:FPC], both[FPC:FPC + 1]
        else:
            col = exchange(n, pad8(col))[:FPC]
        occ = jnp.broadcast_to(count, col.shape) > 0
        scal = jnp.where(occ, count / FPC / jnp.where(occ, col, 1.0), 0.0)
        hi = scal.astype(BF16)
        lo = (scal - hi.astype(F32)).astype(BF16)
        mass = jnp.zeros((FPC, width_m), F32)
        for c in range(nch):
            m = member[:, piece(c)]
            sw = jnp.dot(hi, m, preferred_element_type=F32) + jnp.dot(lo, m, preferred_element_type=F32)
            ks = kern_of(c) * sw
            row = jnp.sum(ks, axis=0, keepdims=True)
            lv = livef[:, piece(c)] > 0
            weights[c] = jnp.where(lv, 1.0 / jnp.where(lv, row, 1.0), 0.0)
            if n == ITERS - 1:
                low = (ks * weights[c]).astype(BF16)
                plan_ref[:, piece(c)] = low
                mass = mass + lax.dot_general(low, m, NT, preferred_element_type=F32)
    mass_ref[...] = exchange(ITERS, pad8(mass))[:FPC]


def update_kernel(groups, protos, reps, cap, fw, plan_ref, slot_ref, r_ref, mass_ref, proto_ref, dest_ref,
                  new_ref, codes_ref, send, mrec, crec, ss, ssr,
                  csem, crsem, msem, mrsem, lsem, ssem, ssrsem):
    mg, mp, mr = lax.axis_index("group"), lax.axis_index("proto"), lax.axis_index("rep")
    total = groups * cap
    fine = FPC // protos
    packed = send.shape[1]
    width = send.shape[2]
    wide = r_ref.shape[1]
    off = width - wide
    shift = width // 2 - off
    share = protos // reps
    half_to = lax.rem(mp, reps)
    j_mine = mp // reps
    peers = others("group")
    for a in range(reps):
        for b in range(protos):
            if a or b:
                peers.append({"rep": lax.rem(mr + a, reps), "proto": lax.rem(mp + b, protos)})
    greet(peers)
    copies = []
    f_rows = pl.ds(pl.multiple_of(mp * fine, fine), fine)
    for k in range(1, groups):
        to = lax.rem(mg + k, groups)
        c = remote(plan_ref.at[f_rows, pl.ds(pl.multiple_of(to * cap, cap), cap)], crec.at[mg],
                   csem.at[k], crsem.at[k], {"group": to})
        c.start()
        copies.append(c)
    crec_own = plan_ref[f_rows, pl.ds(pl.multiple_of(mg * cap, cap), cap)]
    crec[mg] = crec_own

    block = 256
    per = block // fine
    chunk = 1024
    slotf = slot_ref[:1, :].astype(F32)
    lane = lax.broadcasted_iota(jnp.int32, (block, off), 1)

    def moment(to, first_cluster):
        first = lax.convert_element_type(first_cluster, F32)
        plan_rows = pl.ds(pl.multiple_of(to * fine, fine), fine)
        acc = jnp.zeros((block, wide), F32)
        for c in range(total // chunk):
            lanes = slice(c * chunk, (c + 1) * chunk)
            plan = plan_ref[plan_rows, lanes]
            slots = (jnp.broadcast_to(slotf[:, lanes], (fine, chunk)) - first).astype(BF16)
            a = jnp.concatenate(
                [jnp.where(slots == jnp.asarray(i + 1, BF16), plan, jnp.zeros((), BF16)) for i in range(per)], axis=0)
            acc = acc + jnp.dot(a, r_ref[lanes, :], preferred_element_type=F32)
        return acc

    slot_out = mr * share + j_mine
    is_self = half_to == mr
    mcopies = []
    for k in list(range(1, protos)) + [0]:
        to = lax.rem(mp + k, protos)

        @pl.loop(0, packed // block)
        def _(t):
            a = moment(to, t * per)
            b = pltpu.roll(moment(to, t * per + packed // fine), shift, 1)
            r = pl.ds(pl.multiple_of(t * block, block), block)
            send[k, r, :off] = a[:, :off].astype(BF16)
            send[k, r, off:wide] = jnp.where(lane < shift, a[:, off:], b[:, :wide - off]).astype(BF16)
            send[k, r, wide:] = b[:, wide - off:].astype(BF16)

        c = remote(send.at[k], mrec.at[slot_out], msem.at[k], mrsem.at[slot_out],
                   {"rep": half_to, "proto": to})
        if k:
            c.start()
            mcopies.append(c)
        else:
            @pl.when(is_self)
            def _():
                l = pltpu.make_async_copy(send.at[0], mrec.at[slot_out], lsem)
                l.start()
                l.wait()

            @pl.when(jnp.logical_not(is_self))
            def _():
                c.start()
                c.wait_send()

    for c in copies:
        c.wait()
    nrow = dest_ref.shape[1]
    rt = 256

    @pl.loop(0, nrow // rt)
    def _(t):
        r = pl.ds(pl.multiple_of(t * rt, rt), rt)
        acc = jnp.zeros((fine, rt), F32)
        d = dest_ref[:, r]
        for g in range(groups):
            at = lax.broadcasted_iota(jnp.int32, (cap, rt), 0) + g * cap
            hot = jnp.where(at == d, 1.0, 0.0).astype(BF16)
            acc = acc + jnp.dot(crec[g], hot, preferred_element_type=F32)
        codes_ref[:, r] = acc * FPC

    for c in mcopies:
        c.wait_send()
    for a in range(reps):
        for j in range(share):
            s = a * share + j
            mine = jnp.logical_and(a == mr, j * reps + mr == mp)

            @pl.when(jnp.logical_not(mine))
            def _():
                remote(send.at[0], mrec.at[s], msem.at[0], mrsem.at[s],
                       {"rep": lax.rem(mr + 1, reps)}).wait_recv()

    lane2 = lax.broadcasted_iota(jnp.int32, (128, off), 1)
    eye = lax.broadcasted_iota(jnp.int32, (128, 128), 0) == lax.broadcasted_iota(jnp.int32, (128, 128), 1)
    n128 = packed // 128
    mass_mine = jnp.concatenate([mass_ref[f_rows, :]] * (128 // fine), axis=0)
    cl_lane = lax.broadcasted_iota(jnp.int32, (128, 128), 1) - lax.broadcasted_iota(jnp.int32, (128, 128), 0) // fine

    def mass_of(t):
        return jnp.sum(jnp.where(cl_lane == t * (128 // fine), mass_mine, 0.0), axis=1, keepdims=True)

    sums = []
    for t in range(n128):
        r = slice(t * 128, (t + 1) * 128)
        v = []
        for j in range(share):
            x = mrec[j, r, :].astype(F32)
            for a in range(1, reps):
                x = x + mrec[a * share + j, r, :].astype(F32)
            v.append(x)
        t0, t1 = v
        b = pltpu.roll(t1[:, :wide], shift, 1)
        u = pltpu.roll(t0[:, off:], wide - shift, 1)
        first = [t0[:, :off], jnp.where(lane2 < shift, t0[:, off:wide], b[:, :wide - off]), b[:, wide - off:]]
        second = [u[:, :off], jnp.where(lane2 < shift, u[:, off:wide], t1[:, off:wide]), t1[:, wide:]]
        for h, vals in enumerate((first, second)):
            rr = slice(h * packed + t * 128, h * packed + (t + 1) * 128)
            mom = jnp.concatenate(vals, axis=1)
            up = (proto_ref[rr, :].astype(F32) + mom) / (1.0 + mass_of(h * n128 + t))
            new_ref[rr, :] = up
            q = jnp.sum(up * up, axis=1, keepdims=True)
            sums.append((h * n128 + t, jnp.sum(jnp.where(eye, jnp.broadcast_to(q, (128, 128)), 0.0), axis=0, keepdims=True)))
    sums.sort(key=lambda e: e[0])
    own = jnp.concatenate([e[1] for e in sums], axis=0)
    ss[...] = own
    cs = []
    for k in range(1, reps):
        c = remote(ss, ssr.at[k], ssem.at[k], ssrsem.at[k], {"rep": lax.rem(mr + k, reps)})
        c.start()
        cs.append(c)
    for k in range(1, reps):
        cs[k - 1].wait()
        own = own + ssr[k]
    inv = lax.rsqrt(own / (fw * protos) + 1e-06)
    for t in range(2 * n128):
        rr = slice(t * 128, (t + 1) * 128)
        f = jnp.sum(jnp.where(eye, jnp.broadcast_to(inv[t:t + 1, :], (128, 128)), 0.0), axis=1, keepdims=True)
        new_ref[rr, :] = new_ref[rr, :] * f


def body(embeddings, labels, cluster_place, row_counts, prototypes):
    rows, dim = embeddings.shape
    groups, protos, reps = lax.axis_size("group"), lax.axis_size("proto"), lax.axis_size("rep")
    mp, mr = lax.axis_index("proto"), lax.axis_index("rep")
    cap = rows // max(groups // 4, 2)
    clusters, fine, _ = prototypes.shape
    share = protos // reps
    fw = dim // protos
    wide = -(-fw // 128) * 128
    width = 2 * fw
    off = width - wide
    half = cap // 2
    tile = min(256, half)
    total = groups * cap
    cols = clusters * fine

    place = jnp.sum(jnp.where(labels[:, None] == jnp.arange(cluster_place.shape[0])[None, :],
                              cluster_place[None, :], 0), axis=1)
    target, slot = place // clusters, place % clusters
    live = jnp.arange(rows) < row_counts[0]
    choose = (target[:, None] == jnp.arange(groups)[None, :]) & live[:, None]
    running = jnp.cumsum(choose.astype(jnp.int32), axis=0) - 1
    position = jnp.sum(jnp.where(choose, running, 0), axis=1)
    dest = jnp.where(live, target * cap + position, -1).astype(jnp.int32)
    slot16 = jnp.broadcast_to((slot + 1).astype(BF16)[None, :], (16, rows))
    rows_f = embeddings.astype(F32)
    inv = lax.rsqrt(jnp.mean(rows_f * rows_f, axis=-1, keepdims=True) + 1e-06)
    q = lax.rem(mp, reps) * share + mp // reps
    mine = lax.dynamic_slice_in_dim(embeddings, q * fw, fw, 1).astype(F32)
    xq = (mine * inv).astype(BF16)
    xa = jnp.pad(xq, ((0, 0), (0, wide - fw)))
    xb = jnp.pad(xq, ((0, 0), (wide - fw, 0)))
    dma, sds = pltpu.SemaphoreType.DMA, jax.ShapeDtypeStruct
    params = functools.partial(pltpu.CompilerParams, has_side_effects=True, vmem_limit_bytes=60 * 2**20)
    plan, mass, slots, r = pl.pallas_call(
        functools.partial(sinkhorn_kernel, groups, protos, reps, cap, tile, width, fw, 1.0 / (dim * SHARPNESS)),
        out_shape=(sds((FPC, total), BF16), sds((FPC, 128), F32), sds((8, total), jnp.int32),
                   sds((total, wide), BF16)),
        in_specs=[VM] * 5,
        out_specs=(VM,) * 4,
        scratch_shapes=[pltpu.VMEM((groups, half + EXTRA, width), BF16),
                        pltpu.VMEM((groups, half + EXTRA, width), BF16),
                        pltpu.VMEM((protos, cols // 2, width), BF16),
                        pltpu.VMEM((protos, cols // 2, width), BF16),
                        pltpu.VMEM((protos, cols, wide), BF16),
                        pltpu.VMEM((protos, fine, total), F32), pltpu.VMEM((protos, fine, total), F32),
                        pltpu.VMEM((128, total), BF16),
                        pltpu.VMEM((ITERS + 1, FPC + 8, 128), F32),
                        pltpu.VMEM((ITERS + 1, reps, FPC + 8, 128), F32),
                        pltpu.VMEM((protos, fine, total), BF16),
                        dma((groups,)), dma((groups,)), dma((protos,)), dma((protos,)),
                        dma((groups, protos)), dma((groups, protos)), dma((groups, protos)), dma((groups, protos)),
                        dma((ITERS + 1, reps)), dma((ITERS + 1, reps))],
        compiler_params=params(collective_id=0),
    )(dest[None, :], slot16, xa, xb, prototypes.reshape(cols, dim))
    hw = dim // reps
    proto_half = lax.dynamic_slice_in_dim(prototypes, mr * hw, hw, 2).reshape(cols, hw)
    new, codes = pl.pallas_call(
        functools.partial(update_kernel, groups, protos, reps, cap, fw),
        out_shape=(sds((cols, hw), F32), sds((fine, rows), F32)),
        in_specs=[VM] * 6,
        out_specs=(VM, VM),
        scratch_shapes=[pltpu.VMEM((protos, cols // 2, width), BF16),
                        pltpu.VMEM((reps * share, cols // 2, width), BF16),
                        pltpu.VMEM((groups, fine, cap), BF16),
                        pltpu.VMEM((cols // 128, 128), F32), pltpu.VMEM((reps, cols // 128, 128), F32),
                        dma((groups,)), dma((groups,)), dma((protos,)), dma((reps * share,)), dma,
                        dma((reps,)), dma((reps,))],
        compiler_params=params(collective_id=1),
    )(plan, slots, r, mass, proto_half, dest[None, :])
    return new.reshape(clusters, fine, hw), codes.T


def solution(mesh):
    return jax.shard_map(
        body,
        mesh=mesh,
        in_specs=(
            P(("rep", "group"), None),
            P(("rep", "group")),
            P(),
            P(("rep", "group")),
            P("group", "proto", None),
        ),
        out_specs=(P("group", "proto", "rep"), P(("rep", "group"), "proto")),
        check_vma=False,
    )
```

```python
import functools

import jax
import jax.numpy as jnp
from jax import lax
from jax.experimental import pallas as pl
from jax.experimental.pallas import tpu as pltpu
from jax.sharding import PartitionSpec as P

FPC = 64
ITERS = 3
SHARPNESS = 0.03
EXTRA = 16
F32, BF16 = jnp.float32, jnp.bfloat16
MESH = pl.DeviceIdType.MESH
VM = pl.BlockSpec(memory_space=pltpu.VMEM)
NT = (((1,), (1,)), ((), ()))


def unit(values):
    return values * lax.rsqrt(jnp.mean(values * values, axis=-1, keepdims=True) + 1e-06)


def remote(src, dst, send_sem, recv_sem, where):
    return pltpu.make_async_remote_copy(
        src_ref=src, dst_ref=dst, send_sem=send_sem, recv_sem=recv_sem,
        device_id=where, device_id_type=MESH)


def greet(peers):
    barrier = pltpu.get_barrier_semaphore()
    for peer in peers:
        pl.semaphore_signal(barrier, inc=1, device_id=peer, device_id_type=MESH)
    pl.semaphore_wait(barrier, len(peers))


def others(name):
    n, me = lax.axis_size(name), lax.axis_index(name)
    return [{name: lax.rem(me + k, n)} for k in range(1, n)]


def sinkhorn_kernel(groups, protos, reps, cap, tile, width, fw, scale,
                    dest_ref, slot_in_ref, xa_ref, proto_ref,
                    plan_ref, mass_ref, slot_ref, r_ref,
                    got, send, wsend, wgot, w_ref, part, prec, member, xs, xr, kall,
                    ssem, rsem, wssem, wrsem, psem, prsem, ksem, krsem, xsem, xrsem):
    me, mp, mr = lax.axis_index("group"), lax.axis_index("proto"), lax.axis_index("rep")
    half = cap // 2
    total = groups * cap
    wide = r_ref.shape[1]
    off = width - wide
    shift = fw - off
    cols, dim = proto_ref.shape
    fine = FPC // protos
    share = protos // reps
    rows = dest_ref.shape[1]
    row16 = lax.broadcasted_iota(jnp.int32, (EXTRA, tile), 0)
    greet(others("group") + others("proto") + others("rep"))

    def bucket(k):
        to = lax.rem(me + k, groups)
        buf = got.at[me] if k == 0 else send.at[k]
        codes = jnp.zeros((EXTRA, tile), F32)
        for t in range(half // tile):
            at = lax.broadcasted_iota(jnp.int32, (tile, rows), 0) + (to * cap + t * tile)
            oa = jnp.where(at == dest_ref[...], 1.0, 0.0).astype(BF16)
            ob = jnp.where(at + half == dest_ref[...], 1.0, 0.0).astype(BF16)
            a = jnp.dot(oa, xa_ref[...], preferred_element_type=F32)
            b = pltpu.roll(jnp.dot(ob, xa_ref[...], preferred_element_type=F32), shift, 1)
            sa = lax.dot_general(slot_in_ref[...], oa, NT, preferred_element_type=F32)
            sb = lax.dot_general(slot_in_ref[...], ob, NT, preferred_element_type=F32)
            codes = jnp.where(row16 == t, sa, codes)
            codes = jnp.where(row16 == half // tile + t, sb, codes)
            r = pl.ds(t * tile, tile)
            buf[r, :off] = a[:, :off].astype(BF16)
            buf[r, off:wide] = (a[:, off:] + b[:, :wide - off]).astype(BF16)
            buf[r, wide:] = b[:, wide - off:].astype(BF16)
        buf[pl.ds(half, EXTRA), :tile] = codes.astype(BF16)
        buf[pl.ds(half, EXTRA), tile:] = jnp.zeros((EXTRA, width - tile), BF16)
        if k:
            c = remote(send.at[k], got.at[me], ssem.at[k], rsem.at[k], {"group": to})
            c.start()
            return c

    def spread_protos():
        wt = 128
        lane = lax.broadcasted_iota(jnp.int32, (wt, off), 1)

        @pl.loop(0, cols // 2 // wt)
        def _(t):
            ra = pl.ds(pl.multiple_of(t * wt, wt), wt)
            rb = pl.ds(pl.multiple_of(t * wt + cols // 2, wt), wt)
            ua, ub = unit(proto_ref[ra, :].astype(F32)), unit(proto_ref[rb, :].astype(F32))
            for q in range(protos):
                p = (q % share) * reps + q // share
                base = q * fw // 128 * 128
                o = q * fw - base
                a, b = ua[:, base:base + wide], ub[:, base:base + wide]
                a = a if o == 0 else pltpu.roll(a, wide - o, 1)
                b = b if o == shift else pltpu.roll(b, (shift - o) % wide, 1)
                wsend[p, ra, :off] = a[:, :off].astype(BF16)
                wsend[p, ra, off:wide] = jnp.where(lane < shift, a[:, off:], b[:, :wide - off]).astype(BF16)
                wsend[p, ra, wide:] = b[:, wide - off:].astype(BF16)
        cs = []
        for k in range(1, protos):
            to = lax.rem(mp + k, protos)
            c = remote(wsend.at[to], wgot.at[k], wssem.at[k], wrsem.at[k], {"proto": to})
            c.start()
            cs.append(c)
        return cs

    order = [groups // 2] + [k for k in range(1, groups) if k != groups // 2]
    sent = {order[0]: bucket(order[0])}
    wcopies = spread_protos()
    for k in order[1:]:
        sent[k] = bucket(k)
    bucket(0)

    keep = lax.broadcasted_iota(jnp.int32, (cols // 2, wide), 1) < fw
    for k in range(protos):
        if k:
            wcopies[k - 1].wait()
        src = wsend.at[mp] if k == 0 else wgot.at[k]
        w_ref[k, :cols // 2, :] = jnp.where(keep, src[:, :wide].astype(F32), 0.0).astype(BF16)
        b = pltpu.roll(src[:, off:].astype(F32), wide - shift, 1)
        w_ref[k, cols // 2:, :] = jnp.where(keep, b, 0.0).astype(BF16)

    chunk = 512
    step = 256
    per = step // fine
    width_m = member.shape[0]
    cl = lax.broadcasted_iota(jnp.int32, (width_m, cap), 0) + 1

    def lanes_of(k):
        src = lax.rem(me - k + groups, groups)
        return src, pl.ds(pl.multiple_of(src * cap, cap), cap)

    def score(k):
        src, lanes = lanes_of(k)
        if k:
            sent[k].wait()
        base = src * cap
        r_ref[pl.ds(pl.multiple_of(base, half), half), :] = got[src, :half, :wide]
        b = got[src, :half, off:].astype(F32)
        r_ref[pl.ds(pl.multiple_of(base + half, half), half), :] = pltpu.roll(b, wide - shift, 1).astype(BF16)
        codes = got[src, pl.ds(half, EXTRA), :tile].astype(F32)
        slots = jnp.concatenate([codes[u:u + 1, :] for u in range(cap // tile)], axis=1)
        slots = jnp.broadcast_to(slots, (8, cap)).astype(jnp.int32)
        slot_ref[:, lanes] = slots
        member[:, lanes] = jnp.where(slots[:1] == cl, 1.0, 0.0).astype(BF16)

        @pl.loop(0, cap // chunk)
        def _(c):
            at = pl.ds(pl.multiple_of(base + c * chunk, chunk), chunk)
            x = r_ref[at, :]
            sl = slot_ref[:, at]
            acc = [[jnp.zeros((8, chunk), F32) for _ in range(fine // 8)] for _ in range(protos)]
            for j in range(cols // step):
                for p in range(protos):
                    s = lax.dot_general(w_ref[p, j * step:(j + 1) * step, :], x, NT, preferred_element_type=F32)
                    for i in range(per):
                        hit = sl == j * per + i + 1
                        for h in range(fine // 8):
                            z = i * fine + h * 8
                            acc[p][h] = jnp.where(hit, s[z:z + 8], acc[p][h])
            for p in range(protos):
                part[p, :, at] = jnp.concatenate(acc[p], axis=0)

        cs = []
        for p in range(1, protos):
            to = lax.rem(mp - p + protos, protos)
            c = remote(part.at[p, :, lanes], prec.at[p, :, lanes], psem.at[k, p], prsem.at[k, p], {"proto": to})
            c.start()
            cs.append(c)
        return cs

    def finish(k, cs):
        _, lanes = lanes_of(k)
        for c in cs:
            c.wait()
        s = part[0, :, lanes]
        for p in range(1, protos):
            s = s + prec[p, :, lanes]
        live = jnp.broadcast_to(slot_ref[:1, lanes], s.shape) > 0
        kall[mp, :, lanes] = jnp.where(live, jnp.exp(s * scale), 0.0).astype(BF16)
        out = []
        for p in range(1, protos):
            to = lax.rem(mp + p, protos)
            c = remote(kall.at[mp, :, lanes], kall.at[mp, :, lanes], ksem.at[k, p], krsem.at[k, p], {"proto": to})
            c.start()
            out.append(c)
        return out

    pending, last = [], None
    for k in [0] + order:
        now = (k, score(k))
        if last is not None:
            pending += finish(*last)
        last = now
    pending += finish(*last)

    def exchange(n, value):
        xs[n] = value
        cs = []
        for k in range(1, reps):
            to = lax.rem(mr + k, reps)
            c = remote(xs.at[n], xr.at[n, k], xsem.at[n, k], xrsem.at[n, k], {"rep": to})
            c.start()
            cs.append(c)
        for k in range(1, reps):
            cs[k - 1].wait()
            value = value + xr[n, k]
        return value

    def pad8(v):
        return jnp.concatenate([v, jnp.zeros((8, width_m), F32)], axis=0)

    nch = total // chunk
    livef = (slot_ref[:1, :] > 0).astype(F32)

    def piece(c):
        return slice(c * chunk, (c + 1) * chunk)

    def kern_of(c):
        return kall[:, :, piece(c)].reshape(FPC, chunk).astype(F32)

    weights = [livef[:, piece(c)] for c in range(nch)]
    counts = lax.dot_general(jnp.broadcast_to(livef, (16, total)).astype(BF16), member[...], NT,
                             preferred_element_type=F32)[:8]
    for c in pending:
        c.wait()
    for n in range(ITERS):
        col = jnp.zeros((FPC, width_m), F32)
        for c in range(nch):
            kw = (kern_of(c) * weights[c]).astype(BF16)
            col = col + lax.dot_general(kw, member[:, piece(c)], NT, preferred_element_type=F32)
        if n == 0:
            both = exchange(0, jnp.concatenate([col, counts], axis=0))
            col, count = both[:FPC], both[FPC:FPC + 1]
        else:
            col = exchange(n, pad8(col))[:FPC]
        occ = jnp.broadcast_to(count, col.shape) > 0
        scal = jnp.where(occ, count / FPC / jnp.where(occ, col, 1.0), 0.0)
        hi = scal.astype(BF16)
        lo = (scal - hi.astype(F32)).astype(BF16)
        mass = jnp.zeros((FPC, width_m), F32)
        for c in range(nch):
            m = member[:, piece(c)]
            sw = jnp.dot(hi, m, preferred_element_type=F32) + jnp.dot(lo, m, preferred_element_type=F32)
            ks = kern_of(c) * sw
            row = jnp.sum(ks, axis=0, keepdims=True)
            lv = livef[:, piece(c)] > 0
            weights[c] = jnp.where(lv, 1.0 / jnp.where(lv, row, 1.0), 0.0)
            if n == ITERS - 1:
                low = (ks * weights[c]).astype(BF16)
                plan_ref[:, piece(c)] = low
                mass = mass + lax.dot_general(low, m, NT, preferred_element_type=F32)
    mass_ref[...] = mass


def update_kernel(groups, protos, reps, cap, fw, plan_ref, slot_ref, r_ref, mass_ref, proto_ref, dest_ref,
                  new_ref, codes_ref, send, mrec, crec, ss, ssr,
                  csem, crsem, msem, mrsem, lsem, ssem, ssrsem, mx, mxsem, mxrsem):
    mg, mp, mr = lax.axis_index("group"), lax.axis_index("proto"), lax.axis_index("rep")
    total = groups * cap
    fine = FPC // protos
    packed = send.shape[1]
    width = send.shape[2]
    wide = r_ref.shape[1]
    off = width - wide
    shift = width // 2 - off
    share = protos // reps
    half_to = lax.rem(mp, reps)
    j_mine = mp // reps
    peers = others("group")
    for a in range(reps):
        for b in range(protos):
            if a or b:
                peers.append({"rep": lax.rem(mr + a, reps), "proto": lax.rem(mp + b, protos)})
    greet(peers)
    copies = []
    f_rows = pl.ds(pl.multiple_of(mp * fine, fine), fine)
    for k in range(1, groups):
        to = lax.rem(mg + k, groups)
        c = remote(plan_ref.at[f_rows, pl.ds(pl.multiple_of(to * cap, cap), cap)], crec.at[mg],
                   csem.at[k], crsem.at[k], {"group": to})
        c.start()
        copies.append(c)
    mass_copies = []
    for k in range(1, reps):
        c = remote(mass_ref, mx.at[k], mxsem.at[k], mxrsem.at[k], {"rep": lax.rem(mr + k, reps)})
        c.start()
        mass_copies.append(c)
    crec_own = plan_ref[f_rows, pl.ds(pl.multiple_of(mg * cap, cap), cap)]
    crec[mg] = crec_own

    block = 256
    per = block // fine
    chunk = 1024
    slotf = slot_ref[:1, :].astype(F32)
    lane = lax.broadcasted_iota(jnp.int32, (block, off), 1)

    def moment(to, first_cluster):
        first = lax.convert_element_type(first_cluster, F32)
        plan_rows = pl.ds(pl.multiple_of(to * fine, fine), fine)
        acc = jnp.zeros((block, wide), F32)
        for c in range(total // chunk):
            lanes = slice(c * chunk, (c + 1) * chunk)
            plan = plan_ref[plan_rows, lanes]
            slots = (jnp.broadcast_to(slotf[:, lanes], (fine, chunk)) - first).astype(BF16)
            a = jnp.concatenate(
                [jnp.where(slots == jnp.asarray(i + 1, BF16), plan, jnp.zeros((), BF16)) for i in range(per)], axis=0)
            acc = acc + jnp.dot(a, r_ref[lanes, :], preferred_element_type=F32)
        return acc

    slot_out = mr * share + j_mine
    is_self = half_to == mr
    mcopies = []
    for k in list(range(1, protos)) + [0]:
        to = lax.rem(mp + k, protos)

        @pl.loop(0, packed // block)
        def _(t):
            a = moment(to, t * per)
            b = pltpu.roll(moment(to, t * per + packed // fine), shift, 1)
            r = pl.ds(pl.multiple_of(t * block, block), block)
            send[k, r, :off] = a[:, :off].astype(BF16)
            send[k, r, off:wide] = jnp.where(lane < shift, a[:, off:], b[:, :wide - off]).astype(BF16)
            send[k, r, wide:] = b[:, wide - off:].astype(BF16)

        c = remote(send.at[k], mrec.at[slot_out], msem.at[k], mrsem.at[slot_out],
                   {"rep": half_to, "proto": to})
        if k:
            c.start()
            mcopies.append(c)
        else:
            @pl.when(is_self)
            def _():
                l = pltpu.make_async_copy(send.at[0], mrec.at[slot_out], lsem)
                l.start()
                l.wait()

            @pl.when(jnp.logical_not(is_self))
            def _():
                c.start()
                c.wait_send()

    for c in copies:
        c.wait()
    nrow = dest_ref.shape[1]
    rt = 256

    @pl.loop(0, nrow // rt)
    def _(t):
        r = pl.ds(pl.multiple_of(t * rt, rt), rt)
        acc = jnp.zeros((fine, rt), F32)
        d = dest_ref[:, r]
        for g in range(groups):
            at = lax.broadcasted_iota(jnp.int32, (cap, rt), 0) + g * cap
            hot = jnp.where(at == d, 1.0, 0.0).astype(BF16)
            acc = acc + jnp.dot(crec[g], hot, preferred_element_type=F32)
        codes_ref[:, r] = acc * FPC

    for c in mcopies:
        c.wait_send()
    for a in range(reps):
        for j in range(share):
            s = a * share + j
            mine = jnp.logical_and(a == mr, j * reps + mr == mp)

            @pl.when(jnp.logical_not(mine))
            def _():
                remote(send.at[0], mrec.at[s], msem.at[0], mrsem.at[s],
                       {"rep": lax.rem(mr + 1, reps)}).wait_recv()

    lane2 = lax.broadcasted_iota(jnp.int32, (128, off), 1)
    eye = lax.broadcasted_iota(jnp.int32, (128, 128), 0) == lax.broadcasted_iota(jnp.int32, (128, 128), 1)
    n128 = packed // 128
    hw = new_ref.shape[1]
    half_lanes = pl.ds(pl.multiple_of(mr * hw, 128), hw)
    mass_f = mass_ref[f_rows, :]
    for k in range(1, reps):
        mass_copies[k - 1].wait()
        mass_f = mass_f + mx[k, f_rows, :]
    mass_mine = jnp.concatenate([mass_f] * (128 // fine), axis=0)
    cl_lane = lax.broadcasted_iota(jnp.int32, (128, 128), 1) - lax.broadcasted_iota(jnp.int32, (128, 128), 0) // fine

    def mass_of(t):
        return jnp.sum(jnp.where(cl_lane == t * (128 // fine), mass_mine, 0.0), axis=1, keepdims=True)

    sums = []
    for t in range(n128):
        r = slice(t * 128, (t + 1) * 128)
        v = []
        for j in range(share):
            x = mrec[j, r, :].astype(F32)
            for a in range(1, reps):
                x = x + mrec[a * share + j, r, :].astype(F32)
            v.append(x)
        t0, t1 = v
        b = pltpu.roll(t1[:, :wide], shift, 1)
        u = pltpu.roll(t0[:, off:], wide - shift, 1)
        first = [t0[:, :off], jnp.where(lane2 < shift, t0[:, off:wide], b[:, :wide - off]), b[:, wide - off:]]
        second = [u[:, :off], jnp.where(lane2 < shift, u[:, off:wide], t1[:, off:wide]), t1[:, wide:]]
        for h, vals in enumerate((first, second)):
            rr = slice(h * packed + t * 128, h * packed + (t + 1) * 128)
            mom = jnp.concatenate(vals, axis=1)
            up = (proto_ref[rr, half_lanes].astype(F32) + mom) / (1.0 + mass_of(h * n128 + t))
            new_ref[rr, :] = up
            q = jnp.sum(up * up, axis=1, keepdims=True)
            sums.append((h * n128 + t, jnp.sum(jnp.where(eye, jnp.broadcast_to(q, (128, 128)), 0.0), axis=0, keepdims=True)))
    sums.sort(key=lambda e: e[0])
    own = jnp.concatenate([e[1] for e in sums], axis=0)
    ss[...] = own
    cs = []
    for k in range(1, reps):
        c = remote(ss, ssr.at[k], ssem.at[k], ssrsem.at[k], {"rep": lax.rem(mr + k, reps)})
        c.start()
        cs.append(c)
    for k in range(1, reps):
        cs[k - 1].wait()
        own = own + ssr[k]
    inv = lax.rsqrt(own / (fw * protos) + 1e-06)
    for t in range(2 * n128):
        rr = slice(t * 128, (t + 1) * 128)
        f = jnp.sum(jnp.where(eye, jnp.broadcast_to(inv[t:t + 1, :], (128, 128)), 0.0), axis=1, keepdims=True)
        new_ref[rr, :] = new_ref[rr, :] * f


def body(embeddings, labels, cluster_place, row_counts, prototypes):
    rows, dim = embeddings.shape
    groups, protos, reps = lax.axis_size("group"), lax.axis_size("proto"), lax.axis_size("rep")
    mp, mr = lax.axis_index("proto"), lax.axis_index("rep")
    cap = rows // max(groups // 4, 2)
    clusters, fine, _ = prototypes.shape
    share = protos // reps
    fw = dim // protos
    wide = -(-fw // 128) * 128
    width = 2 * fw
    off = width - wide
    half = cap // 2
    tile = min(256, half)
    total = groups * cap
    cols = clusters * fine

    place = jnp.sum(jnp.where(labels[:, None] == jnp.arange(cluster_place.shape[0])[None, :],
                              cluster_place[None, :], 0), axis=1)
    target, slot = place // clusters, place % clusters
    live = jnp.arange(rows) < row_counts[0]
    choose = (target[:, None] == jnp.arange(groups)[None, :]) & live[:, None]
    running = jnp.cumsum(choose.astype(jnp.int32), axis=0) - 1
    position = jnp.sum(jnp.where(choose, running, 0), axis=1)
    dest = jnp.where(live, target * cap + position, -1).astype(jnp.int32)
    slot16 = jnp.broadcast_to((slot + 1).astype(BF16)[None, :], (16, rows))
    rows_f = embeddings.astype(F32)
    inv = lax.rsqrt(jnp.mean(rows_f * rows_f, axis=-1, keepdims=True) + 1e-06)
    q = lax.rem(mp, reps) * share + mp // reps
    mine = lax.dynamic_slice_in_dim(embeddings, q * fw, fw, 1).astype(F32)
    xq = (mine * inv).astype(BF16)
    xa = jnp.pad(xq, ((0, 0), (0, wide - fw)))
    dma, sds = pltpu.SemaphoreType.DMA, jax.ShapeDtypeStruct
    params = functools.partial(pltpu.CompilerParams, has_side_effects=True, vmem_limit_bytes=60 * 2**20)
    plan, mass, slots, r = pl.pallas_call(
        functools.partial(sinkhorn_kernel, groups, protos, reps, cap, tile, width, fw, 1.0 / (dim * SHARPNESS)),
        out_shape=(sds((FPC, total), BF16), sds((FPC, 128), F32), sds((8, total), jnp.int32),
                   sds((total, wide), BF16)),
        in_specs=[VM] * 4,
        out_specs=(VM,) * 4,
        scratch_shapes=[pltpu.VMEM((groups, half + EXTRA, width), BF16),
                        pltpu.VMEM((groups, half + EXTRA, width), BF16),
                        pltpu.VMEM((protos, cols // 2, width), BF16),
                        pltpu.VMEM((protos, cols // 2, width), BF16),
                        pltpu.VMEM((protos, cols, wide), BF16),
                        pltpu.VMEM((protos, fine, total), F32), pltpu.VMEM((protos, fine, total), F32),
                        pltpu.VMEM((128, total), BF16),
                        pltpu.VMEM((ITERS, FPC + 8, 128), F32),
                        pltpu.VMEM((ITERS, reps, FPC + 8, 128), F32),
                        pltpu.VMEM((protos, fine, total), BF16),
                        dma((groups,)), dma((groups,)), dma((protos,)), dma((protos,)),
                        dma((groups, protos)), dma((groups, protos)), dma((groups, protos)), dma((groups, protos)),
                        dma((ITERS, reps)), dma((ITERS, reps))],
        compiler_params=params(collective_id=0),
    )(dest[None, :], slot16, xa, prototypes.reshape(cols, dim))
    hw = dim // reps
    new, codes = pl.pallas_call(
        functools.partial(update_kernel, groups, protos, reps, cap, fw),
        out_shape=(sds((cols, hw), F32), sds((fine, rows), F32)),
        in_specs=[VM] * 6,
        out_specs=(VM, VM),
        scratch_shapes=[pltpu.VMEM((protos, cols // 2, width), BF16),
                        pltpu.VMEM((reps * share, cols // 2, width), BF16),
                        pltpu.VMEM((groups, fine, cap), BF16),
                        pltpu.VMEM((cols // 128, 128), F32), pltpu.VMEM((reps, cols // 128, 128), F32),
                        dma((groups,)), dma((groups,)), dma((protos,)), dma((reps * share,)), dma,
                        dma((reps,)), dma((reps,)),
                        pltpu.VMEM((reps, FPC, 128), F32), dma((reps,)), dma((reps,))],
        compiler_params=params(collective_id=1),
    )(plan, slots, r, mass, prototypes.reshape(cols, dim), dest[None, :])
    return new.reshape(clusters, fine, hw), codes.T


def solution(mesh):
    return jax.shard_map(
        body,
        mesh=mesh,
        in_specs=(
            P(("rep", "group"), None),
            P(("rep", "group")),
            P(),
            P(("rep", "group")),
            P("group", "proto", None),
        ),
        out_specs=(P("group", "proto", "rep"), P(("rep", "group"), "proto")),
        check_vma=False,
    )
```
